256 devices in a mesh: site: 4 (over x), chan: 32 (over z, y), grp: 2 (over core).
Axes of the slice: x: 4, y: 4, z: 8, core: 2. Of those that a mesh axis runs over, the one named last changes fastest.
Arguments:
- voltages: bfloat16 [2, 65536, 3072], P(None, 'chan', ('site', 'grp')), may hold values from -6 to 6
- taps: float32 [8, 32], replicated, may hold values from -0.375 to 0.375
- sections: int32 [4, 2], replicated, may hold values from 0 to 768, as said below
- tile_list: int32 [2, 68, 2], replicated, may hold values from 0 to 15, as said below
Outputs:
- visibility: float32 [4, 32, 136, 2, 128, 128], P('site', 'chan', 'grp')
The draws below stay inside these ranges and needn't reach their ends.
Inputs may be any that keep to these rules, and one draw needn't show every extreme that they name: `sections`: the live counts sum to 2048; each is at least 128 and at most 768, one site has exactly 768; each first live column plus its count is at most 768. `tile_list`: every pair (p, q) with 0 <= p <= q < 16 stands exactly once in the whole list.
All inputs are finite; a program needn't handle non-finite values.
Results may differ from the reference program's by a relative error of at most 0.0033.
Values may be sent and summed in bfloat16 or wider, within the bound.
No kernel may reach another device: no remote copies, remote signals or barrier semaphores. Data moves between devices by JAX's collectives and lax.ppermute only.
A program may use at most 128 MiB of HBM per device.

```python
import jax
import jax.numpy as jnp
import numpy as np
from jax import lax

NIN = 2048
CAP = 768
PANEL = 128
TAPS = 8
FB = 512
NCHAN = 32
NT = 136
TSLOT = 68
SAMPLES = 65536
N_SITE = 4


def draw_sections(key, part):
    subkeys = jax.random.split(key, 4)
    least = NIN // 16
    remain = NIN - CAP
    first_count = jax.random.randint(subkeys[0], (), max(least, remain - 2 * CAP), min(CAP, remain - 2 * least) + 1)
    second_count = jax.random.randint(subkeys[1], (), jnp.maximum(least, remain - first_count - CAP), jnp.minimum(CAP, remain - first_count - least) + 1)
    third_count = remain - first_count - second_count
    counts = jnp.stack([jnp.int32(CAP), first_count.astype(jnp.int32), second_count.astype(jnp.int32), third_count.astype(jnp.int32)])
    shuffle = jax.random.permutation(subkeys[2], 4)
    counts = counts[shuffle]
    starts = jax.random.randint(subkeys[3], (4,), 0, CAP - counts + 1)
    return jnp.stack([counts, starts.astype(jnp.int32)], axis=1).astype(jnp.int32)


def draw_tile_list(key, part):
    row_panel, col_panel = np.triu_indices(NIN // PANEL)
    pairs = jnp.stack([jnp.asarray(row_panel, jnp.int32), jnp.asarray(col_panel, jnp.int32)], axis=1)
    shuffle = jax.random.permutation(key, pairs.shape[0])
    return pairs[shuffle].reshape(-1, TSLOT, 2).astype(jnp.int32)


def block_scale(stream_key, extent, cuts, low, top_value):
    level = 1.0
    for axis_at, parts in cuts:
        heights = jax.random.uniform(jax.random.fold_in(jax.random.fold_in(stream_key, 6), axis_at), (parts,), jnp.float32, low / len(cuts), top_value / len(cuts))
        level = level * jnp.repeat(jnp.exp(heights), extent[axis_at] // parts).reshape((-1,) + (1,) * (len(extent) - 1 - axis_at))
    return level


def normal_values(own_key, extent, scale, bound, shards=(), kind=jnp.bfloat16):
    values = scale * jax.random.normal(own_key, extent, jnp.float32)
    if shards:
        values = values * block_scale(own_key, extent, shards, -0.22, 0.18)
    return jnp.clip(values, -bound, bound).astype(kind)


def setup_inputs(seed: int = 0) -> dict:
    key_list = jax.random.split(jax.random.key(seed), 5)
    voltages = normal_values(key_list[0], (2, SAMPLES, N_SITE * CAP), 1.0, 6.0, ((1, 32), (2, 8)))
    taps = normal_values(key_list[1], (TAPS, NCHAN), (TAPS * NCHAN) ** -0.5, 0.375, (), jnp.float32)
    sections = draw_sections(jax.random.fold_in(key_list[4], 71), 0)
    tile_list = draw_tile_list(jax.random.fold_in(key_list[4], 71), 0)
    return dict(voltages=voltages, taps=taps, sections=sections, tile_list=tile_list)


def dft_table(chan_count):
    positions = jnp.arange(chan_count, dtype=jnp.int32)
    products = (positions[:, None] * positions[None, :]) % chan_count
    phases = products.astype(jnp.float32) * (2.0 * jnp.pi / chan_count)
    cosine_part = jnp.cos(phases)
    sine_part = jnp.sin(phases)
    from_real = jnp.stack([cosine_part, -sine_part], axis=1)
    from_imag = jnp.stack([sine_part, cosine_part], axis=1)
    return jnp.stack([from_real, from_imag], axis=0)


def filter_frames(history, taps, transform, frames):
    tap_count = taps.shape[0]
    filtered = jnp.zeros((history.shape[0], frames, history.shape[2], history.shape[3]), jnp.float32)
    for tap_index in range(tap_count):
        first_frame = tap_count - 1 - tap_index
        filtered = filtered + taps[tap_index][None, None, :, None] * history[:, first_frame:first_frame + frames]
    spectra = jnp.einsum("qfkr,qkpm->pmfr", filtered, transform, precision=lax.Precision.HIGHEST)
    return spectra.astype(jnp.bfloat16)


def reference(voltages, taps, sections, tile_list):
    chan_count = taps.shape[1]
    frames = voltages.shape[1] // chan_count
    transform = dft_table(chan_count)
    counts = sections[:, 0]
    starts = sections[:, 1]
    offsets = jnp.cumsum(counts) - counts
    inputs = jnp.arange(NIN, dtype=jnp.int32)
    inside = (inputs[:, None] >= offsets[None, :]) & (inputs[:, None] < (offsets + counts)[None, :])
    site_ids = jnp.arange(N_SITE, dtype=jnp.int32)
    in_section = jnp.sum(jnp.where(inside, starts[None, :] + inputs[:, None] - offsets[None, :], 0), axis=1)
    owner_site = jnp.sum(jnp.where(inside, site_ids[None, :], 0), axis=1)
    columns = (owner_site * CAP + in_section).astype(jnp.int32)
    compact = jnp.take(voltages, columns, axis=2)

    def panel_spectra(panel_id):
        panel_block = lax.dynamic_slice_in_dim(compact, (panel_id * PANEL).astype(jnp.int32), PANEL, 2)
        panel_block = panel_block.reshape(2, frames, chan_count, PANEL)
        history = jnp.pad(panel_block.astype(jnp.float32), ((0, 0), (TAPS - 1, 0), (0, 0), (0, 0)))
        return filter_frames(history, taps, transform, frames)

    spectra = lax.map(panel_spectra, jnp.arange(NIN // PANEL, dtype=jnp.int32))
    slot_pairs = tile_list.reshape(-1, 2)

    def add_slot(slot_id, result):
        pair_ids = slot_pairs[slot_id]
        left_panel = spectra[pair_ids[0]].reshape(2, chan_count, N_SITE, FB, PANEL).astype(jnp.float32)
        right_panel = spectra[pair_ids[1]].reshape(2, chan_count, N_SITE, FB, PANEL).astype(jnp.float32)
        gram_block = jnp.einsum("qcbfu,rcbfv->bcqruv", left_panel, right_panel, precision=lax.Precision.HIGHEST)
        real_part = gram_block[:, :, 0, 0] + gram_block[:, :, 1, 1]
        imag_part = gram_block[:, :, 1, 0] - gram_block[:, :, 0, 1]
        tile_value = jnp.stack([real_part, imag_part], axis=2) / FB
        return lax.dynamic_update_slice_in_dim(result, tile_value[:, :, None], slot_id.astype(jnp.int32), 2)

    result = jnp.zeros((N_SITE, chan_count, NT, 2, PANEL, PANEL), jnp.float32)
    return lax.fori_loop(0, NT, add_slot, result)
```

```python
import functools

import jax
import jax.numpy as jnp
import numpy as np
from jax import lax
from jax.experimental import pallas as pl
from jax.experimental.pallas import tpu as pltpu
from jax.sharding import PartitionSpec as P


NIN = 2048
PANEL = 128
PANELS = NIN // PANEL
NCHAN = 32
N_SITE = 4
LOCAL = 64
BLOCKS = 8
FB = LOCAL * BLOCKS
CAP = 768
HALF = 384
TSLOT = 68
TIMES = 4
ROUNDS = 8
SINGLE = 8
PER_STEP = 4
STRIP = 16
GROUP = 8


def trig_rows():
    k = np.arange(NCHAN)
    rows = [np.cos(2.0 * np.pi * (m * k % NCHAN) / NCHAN) for m in range(17)]
    rows += [np.sin(2.0 * np.pi * (m * k % NCHAN) / NCHAN) for m in range(1, 16)]
    return np.tile(np.stack(rows), (1, 2 * GROUP)).astype(np.float32)


def tap_rows(taps):
    flipped = taps[::-1]
    rows = [jnp.pad(flipped, ((j + 1, GROUP - 1 - j), (0, 0))) for j in range(GROUP)]
    return jnp.stack(rows).reshape(GROUP, 2 * GROUP * NCHAN)


def filter_body(slot_of, has_halo, trig_ref, tap_ref, before_ref, now_ref, *rest):
    out_ref, high_ref, low_ref = rest[-3:]

    @pl.when(pl.program_id(0) == 0)
    def _():
        full = (trig_ref[...][:, None, :] * tap_ref[...][None]).reshape(
            NCHAN * GROUP, 2 * GROUP * NCHAN
        )
        high = full.astype(jnp.bfloat16)
        high_ref[...] = high
        low_ref[...] = (full - high.astype(jnp.float32)).astype(jnp.bfloat16)

    step = GROUP * NCHAN
    products = []
    for sub in range(STRIP // GROUP):
        pair = []
        for part in range(2):
            now = now_ref[part]
            if sub == 0:
                before = before_ref[part]
                if has_halo:
                    before = jnp.where(pl.program_id(0) == 0, rest[0][part], before)
                frames = jnp.concatenate([before, now[:step]], axis=0)
            else:
                frames = now
            pair.append(
                jnp.dot(high_ref[...], frames, preferred_element_type=jnp.float32)
                + jnp.dot(low_ref[...], frames, preferred_element_type=jnp.float32)
            )
        products.append(pair)

    def rows(part, index):
        return jnp.concatenate(
            [pair[part][index * GROUP : (index + 1) * GROUP] for pair in products], axis=0
        )

    for m in range(17):
        cos_re, cos_im = rows(0, m), rows(1, m)
        if m in (0, 16):
            out_ref[slot_of(m), 0] = cos_re.astype(jnp.bfloat16)
            out_ref[slot_of(m), 1] = cos_im.astype(jnp.bfloat16)
        else:
            sin_re, sin_im = rows(0, 16 + m), rows(1, 16 + m)
            out_ref[slot_of(m), 0] = (cos_re + sin_im).astype(jnp.bfloat16)
            out_ref[slot_of(m), 1] = (cos_im - sin_re).astype(jnp.bfloat16)
            out_ref[slot_of(NCHAN - m), 0] = (cos_re - sin_im).astype(jnp.bfloat16)
            out_ref[slot_of(NCHAN - m), 1] = (cos_im + sin_re).astype(jnp.bfloat16)


def filter_call(trig, tap_table, voltages, halo, begin, strips, slot_of):
    rows = STRIP * NCHAN
    half_rows = GROUP * NCHAN
    in_specs = [
        pl.BlockSpec((NCHAN, 2 * GROUP * NCHAN), lambda i: (0, 0)),
        pl.BlockSpec((GROUP, 2 * GROUP * NCHAN), lambda i: (0, 0)),
        pl.BlockSpec((2, half_rows, HALF), lambda i: (0, jnp.maximum(2 * (i + begin) - 1, 0), 0)),
        pl.BlockSpec((2, rows, HALF), lambda i: (0, i + begin, 0)),
    ]
    args = [trig, tap_table, voltages, voltages]
    if halo is not None:
        in_specs.append(pl.BlockSpec((2, half_rows, HALF), lambda i: (0, 0, 0)))
        args.append(halo)
    return pl.pallas_call(
        functools.partial(filter_body, slot_of, halo is not None),
        out_shape=jax.ShapeDtypeStruct((NCHAN, 2, STRIP * strips, HALF), jnp.bfloat16),
        grid_spec=pltpu.PrefetchScalarGridSpec(
            num_scalar_prefetch=0,
            grid=(strips,),
            in_specs=in_specs,
            out_specs=pl.BlockSpec((NCHAN, 2, STRIP, HALF), lambda i: (0, 0, i, 0)),
            scratch_shapes=[
                pltpu.VMEM((NCHAN * GROUP, 2 * GROUP * NCHAN), jnp.bfloat16),
                pltpu.VMEM((NCHAN * GROUP, 2 * GROUP * NCHAN), jnp.bfloat16),
            ],
        ),
        compiler_params=pltpu.CompilerParams(vmem_limit_bytes=16 << 20),
        cost_estimate=pl.CostEstimate(
            flops=strips * 2 * 2 * 2 * 2 * 256 * 512 * HALF,
            bytes_accessed=strips * 4 * rows * HALF * 2,
            transcendentals=0,
        ),
    )(*args)


def correlate_body(tiles, sections, place_ref, *refs):
    out_ref, raw_late, raw_soon, lanes, turned, held, in_sems, out_sems = refs[-8:]
    blocks = HALF // PANEL
    frames = BLOCKS * raw_late.shape[4]
    turn, group = place_ref[0], place_ref[1]

    copies = [[], []]
    for index, source in enumerate(refs[: 2 * TIMES]):
        which, step = index // TIMES, index % TIMES
        half = group if which == 0 else 1 - group
        copies[0].append(
            pltpu.make_async_copy(source, raw_late.at[half, step], in_sems.at[0, which, step])
        )
    for index, source in enumerate(refs[2 * TIMES : 2 * TIMES + 2 * ROUNDS]):
        which, step = index // ROUNDS, index % ROUNDS
        half = group if which == 0 else 1 - group
        if step >= SINGLE:
            source = source.at[pl.ds(TIMES, TIMES)]
        copies[1].append(
            pltpu.make_async_copy(
                source, raw_soon.at[half, step % N_SITE, step // N_SITE], in_sems.at[1, which, step]
            )
        )
    for copy in copies[1] + copies[0]:
        copy.start()

    counts = [sections[2 * s] for s in range(N_SITE)]
    starts = [sections[2 * s + 1] for s in range(N_SITE)]
    offsets = [jnp.int32(0)]
    for s in range(N_SITE - 1):
        offsets.append(offsets[-1] + counts[s])

    def pick(values, s):
        got = values[0]
        for index in range(1, N_SITE):
            got = jnp.where(s == index, values[index], got)
        return got

    def fill(chunk, panel):
        low = panel * PANEL
        high = low + PANEL - 1
        s_low = jnp.int32(0)
        s_high = jnp.int32(0)
        for s in range(1, N_SITE):
            s_low = s_low + (low >= offsets[s]).astype(jnp.int32)
            s_high = s_high + (high >= offsets[s]).astype(jnp.int32)
        bound = jnp.where(s_low == s_high, PANEL, pick(offsets, s_high) - low)
        lane = lax.broadcasted_iota(jnp.int32, (frames, PANEL), 1)

        def piece(s, block, part):
            block = jnp.clip(block, 0, 2 * blocks - 1)
            half = block // blocks
            at = pl.multiple_of((block - half * blocks) * PANEL, PANEL)
            slot = (turn - s + N_SITE) % N_SITE
            if chunk == 0:
                value = raw_late[half, :, pl.ds(2 * slot, 2), part, :, pl.ds(at, PANEL)]
            else:
                value = raw_soon[half, slot, :, :, part, :, pl.ds(at, PANEL)]
            return value.reshape(frames, PANEL)

        def window(s, part):
            at = low + pick(starts, s) - pick(offsets, s)
            block, shift = at >> 7, at & 127
            mixed = jnp.where(lane >= shift, piece(s, block, part), piece(s, block + 1, part))
            return pltpu.roll(mixed, (PANEL - shift) & 127, 1)

        def put(part, value):
            span = slice(chunk * frames, (chunk + 1) * frames)
            lanes[panel, span, part * PANEL : (part + 1) * PANEL] = value
            turned[panel, part * PANEL : (part + 1) * PANEL, span] = value.T

        @pl.when(s_low == s_high)
        def _():
            for part in range(2):
                put(part, window(s_low, part))

        @pl.when(s_low != s_high)
        def _():
            for part in range(2):
                put(part, jnp.where(lane < bound, window(s_low, part), window(s_high, part)))

    def repeat(count, action):
        def step(index, carry):
            action(index)
            return carry

        lax.fori_loop(0, count, step, 0)

    for chunk in (1, 0):
        for copy in copies[chunk]:
            copy.wait()
        repeat(PANELS, functools.partial(fill, chunk))

    scale = 1.0 / FB

    def result(at):
        return pltpu.make_async_copy(held.at[at], out_ref.at[0, 0, at], out_sems.at[at])

    def multiply(index):
        base = (group * TSLOT + index * PER_STEP) * 2
        for slot in range(PER_STEP):
            left = turned[tiles[base + 2 * slot]]
            right = lanes[tiles[base + 2 * slot + 1]]
            gram = jnp.dot(left, right, preferred_element_type=jnp.float32)
            at = index * PER_STEP + slot
            held[at, 0] = (gram[:PANEL, :PANEL] + gram[PANEL:, PANEL:]) * scale
            held[at, 1] = (gram[PANEL:, :PANEL] - gram[:PANEL, PANEL:]) * scale
        for slot in range(PER_STEP):
            result(index * PER_STEP + slot).start()

    repeat(TSLOT // PER_STEP, multiply)
    repeat(TSLOT, lambda at: result(at).wait())


def correlate_call(tiles, sections, place, pieces):
    count = pieces[0].shape[2]
    resident = pl.BlockSpec(memory_space=pltpu.HBM)
    return pl.pallas_call(
        correlate_body,
        name="correlate",
        out_shape=jax.ShapeDtypeStruct((1, 1, TSLOT, 2, PANEL, PANEL), jnp.float32),
        grid_spec=pltpu.PrefetchScalarGridSpec(
            num_scalar_prefetch=3,
            grid=(),
            in_specs=[resident] * len(pieces),
            out_specs=resident,
            scratch_shapes=[
                pltpu.VMEM((2, TIMES, ROUNDS, 2, count, HALF), jnp.bfloat16),
                pltpu.VMEM((2, N_SITE, 2, TIMES, 2, count, HALF), jnp.bfloat16),
                pltpu.VMEM((PANELS, FB, 2 * PANEL), jnp.bfloat16),
                pltpu.VMEM((PANELS, 2 * PANEL, FB), jnp.bfloat16),
                pltpu.VMEM((TSLOT, 2, PANEL, PANEL), jnp.float32),
                pltpu.SemaphoreType.DMA((2, 2, ROUNDS)),
                pltpu.SemaphoreType.DMA((TSLOT,)),
            ],
        ),
        compiler_params=pltpu.CompilerParams(vmem_limit_bytes=32 << 20),
        cost_estimate=pl.CostEstimate(
            flops=TSLOT * 2 * 256 * 256 * FB,
            bytes_accessed=TSLOT * 2 * PANEL * PANEL * 4 + 4 * FB * N_SITE * CAP,
            transcendentals=0,
        ),
    )(tiles, sections, place, *pieces)


def move_blocks(keys, sources, shapes, moves):
    def body(key_ref, *refs):
        ins, outs, sems = refs[: len(sources)], refs[len(sources) : -1], refs[-1]

        def at(ref, index):
            where = tuple(key_ref[i[0]] if isinstance(i, tuple) else i for i in index)
            return ref.at[where] if where else ref

        copies = [
            pltpu.make_async_copy(at(ins[i], i_at), at(outs[o], o_at), sems.at[number])
            for number, (i, i_at, o, o_at) in enumerate(moves)
        ]
        for copy in copies:
            copy.start()
        for copy in copies:
            copy.wait()

    return pl.pallas_call(
        body,
        out_shape=[jax.ShapeDtypeStruct(shape, jnp.bfloat16) for shape in shapes],
        grid_spec=pltpu.PrefetchScalarGridSpec(
            num_scalar_prefetch=1,
            grid=(),
            in_specs=[pl.BlockSpec(memory_space=pl.ANY)] * len(sources),
            out_specs=[pl.BlockSpec(memory_space=pl.ANY)] * len(shapes),
            scratch_shapes=[pltpu.SemaphoreType.DMA((len(moves),))],
        ),
        compiler_params=pltpu.CompilerParams(vmem_limit_bytes=1 << 20),
    )(keys, *sources)


def from_behind(value, axis):
    count = lax.axis_size(axis)
    return lax.ppermute(value, axis, [(source, source + 1) for source in range(count - 1)])


def across(turn, flip):
    pairs = []
    for site in range(N_SITE):
        for z in range(8):
            goal = 2 * ((z // 2 + site + turn) % N_SITE) + ((z % 2) ^ flip)
            for y in range(TIMES):
                pairs.append((site * NCHAN + z * TIMES + y, z // 2 * NCHAN + goal * TIMES + y))
    return pairs


def along(step):
    return [(z * TIMES + y, z * TIMES + (y + step) % TIMES) for z in range(8) for y in range(TIMES)]


def swap(piece):
    return lax.ppermute(piece, "grp", [(0, 1), (1, 0)])


def correlator(voltages, taps, sections, tile_list):
    halo = from_behind(voltages[:, -GROUP * NCHAN :], "chan")
    trig = jnp.asarray(trig_rows())
    tap_table = tap_rows(taps)
    site, chan, group = (lax.axis_index(name) for name in ("site", "chan", "grp"))
    z, y = chan // TIMES, chan % TIMES
    place = jnp.stack([(z // 2 - site) % N_SITE, group])
    tiles, section_list = tile_list.reshape(-1), sections.reshape(-1)
    strips = LOCAL // STRIP // 2
    rounds = [(turn, flip) for flip in range(2) for turn in range(N_SITE)]
    goals = [2 * ((z // 2 + site + turn) % N_SITE) + ((z % 2) ^ flip) for turn, flip in rounds]
    keys = jnp.stack(goals + [(y + step) % TIMES for step in range(TIMES)])
    joint = ("site", "chan")
    block = (2, STRIP * strips, HALF)

    soon = filter_call(
        trig, tap_table, voltages, None, strips, strips, lambda m: m % TIMES * 8 + m // TIMES
    ).reshape((TIMES, 8) + block)
    held = []
    for step in range(TIMES):
        piece = lax.dynamic_index_in_dim(soon, (y + step) % TIMES, 0, keepdims=False)
        if step:
            piece = lax.ppermute(piece, "chan", along(step))
        held.append(piece)

    late = filter_call(trig, tap_table, voltages, halo, 0, strips, lambda m: m)
    late = late.reshape((8, TIMES) + block)
    late_got, soon_own = [None] * ROUNDS, [None] * ROUNDS
    for index in range(SINGLE):
        piece = lax.dynamic_index_in_dim(late, goals[index], 0, keepdims=False)
        late_got[index] = lax.ppermute(piece, joint, across(*rounds[index]))

    moves, shapes = [], []
    for index in list(range(SINGLE, ROUNDS)) + list(range(SINGLE)):
        both = index >= SINGLE
        if both:
            moves += [(TIMES, ((index,), part), len(shapes), (part,)) for part in range(TIMES)]
        moves += [
            (step, ((index,),), len(shapes), (TIMES * both + step,)) for step in range(TIMES)
        ]
        shapes.append((TIMES * (1 + both),) + block)
    ready = move_blocks(keys, held, shapes, moves)
    for number, piece in enumerate(ready):
        index = (number + SINGLE) % ROUNDS
        soon_own[index] = lax.ppermute(piece, joint, across(*rounds[index]))
        if index >= SINGLE:
            late_got[index] = soon_own[index]

    moves = [
        (index, ((ROUNDS + step,),), step, (index % N_SITE * 2 + index // N_SITE,))
        for step in range(TIMES)
        for index in range(ROUNDS)
    ]
    shapes = [(ROUNDS,) + block] * TIMES
    late_own = list(move_blocks(keys, late_got, shapes, moves))
    for step in range(1, TIMES):
        late_own[step] = lax.ppermute(late_own[step], "chan", along(step))

    pieces = []
    for own in (late_own, soon_own):
        pieces += own + [swap(piece) for piece in own]
    return correlate_call(tiles, section_list, place, pieces)


def solution(mesh):
    in_specs = (P(None, "chan", ("site", "grp")), P(), P(), P())
    out_specs = P("site", "chan", "grp", None, None, None)
    return jax.shard_map(
        correlator, mesh=mesh, in_specs=in_specs, out_specs=out_specs, check_vma=False
    )
```

```python
import functools

import jax
import jax.numpy as jnp
import numpy as np
from jax import lax
from jax.experimental import pallas as pl
from jax.experimental.pallas import tpu as pltpu
from jax.sharding import PartitionSpec as P


NIN = 2048
PANEL = 128
PANELS = NIN // PANEL
NCHAN = 32
N_SITE = 4
LOCAL = 64
BLOCKS = 8
FB = LOCAL * BLOCKS
CAP = 768
HALF = 384
TSLOT = 68
TIMES = 4
PER_STEP = 17
STRIP = 16
GROUP = 8


def trig_rows():
    k = np.arange(NCHAN)
    rows = [np.cos(2.0 * np.pi * (m * k % NCHAN) / NCHAN) for m in range(17)]
    rows += [np.sin(2.0 * np.pi * (m * k % NCHAN) / NCHAN) for m in range(1, 16)]
    return np.tile(np.stack(rows), (1, 2 * GROUP)).astype(np.float32)


def tap_rows(taps):
    flipped = taps[::-1]
    rows = [jnp.pad(flipped, ((j + 1, GROUP - 1 - j), (0, 0))) for j in range(GROUP)]
    return jnp.stack(rows).reshape(GROUP, 2 * GROUP * NCHAN)


def filter_body(slot_of, has_halo, trig_ref, tap_ref, before_ref, now_ref, *rest):
    out_ref, high_ref, low_ref = rest[-3:]

    @pl.when(pl.program_id(0) == 0)
    def _():
        full = (trig_ref[...][:, None, :] * tap_ref[...][None]).reshape(
            NCHAN * GROUP, 2 * GROUP * NCHAN
        )
        high = full.astype(jnp.bfloat16)
        high_ref[...] = high
        low_ref[...] = (full - high.astype(jnp.float32)).astype(jnp.bfloat16)

    step = GROUP * NCHAN
    products = []
    for sub in range(STRIP // GROUP):
        pair = []
        for part in range(2):
            now = now_ref[part]
            if sub == 0:
                before = before_ref[part]
                if has_halo:
                    before = jnp.where(pl.program_id(0) == 0, rest[0][part], before)
                frames = jnp.concatenate([before, now[:step]], axis=0)
            else:
                frames = now
            pair.append(
                jnp.dot(high_ref[...], frames, preferred_element_type=jnp.float32)
                + jnp.dot(low_ref[...], frames, preferred_element_type=jnp.float32)
            )
        products.append(pair)

    def rows(part, index):
        return jnp.concatenate(
            [pair[part][index * GROUP : (index + 1) * GROUP] for pair in products], axis=0
        )

    for m in range(17):
        cos_re, cos_im = rows(0, m), rows(1, m)
        if m in (0, 16):
            out_ref[slot_of(m), 0] = cos_re.astype(jnp.bfloat16)
            out_ref[slot_of(m), 1] = cos_im.astype(jnp.bfloat16)
        else:
            sin_re, sin_im = rows(0, 16 + m), rows(1, 16 + m)
            out_ref[slot_of(m), 0] = (cos_re + sin_im).astype(jnp.bfloat16)
            out_ref[slot_of(m), 1] = (cos_im - sin_re).astype(jnp.bfloat16)
            out_ref[slot_of(NCHAN - m), 0] = (cos_re - sin_im).astype(jnp.bfloat16)
            out_ref[slot_of(NCHAN - m), 1] = (cos_im + sin_re).astype(jnp.bfloat16)


def filter_call(trig, tap_table, voltages, halo, begin, strips, slot_of):
    rows = STRIP * NCHAN
    half_rows = GROUP * NCHAN
    in_specs = [
        pl.BlockSpec((NCHAN, 2 * GROUP * NCHAN), lambda i: (0, 0)),
        pl.BlockSpec((GROUP, 2 * GROUP * NCHAN), lambda i: (0, 0)),
        pl.BlockSpec((2, half_rows, HALF), lambda i: (0, jnp.maximum(2 * (i + begin) - 1, 0), 0)),
        pl.BlockSpec((2, rows, HALF), lambda i: (0, i + begin, 0)),
    ]
    args = [trig, tap_table, voltages, voltages]
    if halo is not None:
        in_specs.append(pl.BlockSpec((2, half_rows, HALF), lambda i: (0, 0, 0)))
        args.append(halo)
    return pl.pallas_call(
        functools.partial(filter_body, slot_of, halo is not None),
        out_shape=jax.ShapeDtypeStruct((NCHAN, 2, STRIP * strips, HALF), jnp.bfloat16),
        grid_spec=pltpu.PrefetchScalarGridSpec(
            num_scalar_prefetch=0,
            grid=(strips,),
            in_specs=in_specs,
            out_specs=pl.BlockSpec((NCHAN, 2, STRIP, HALF), lambda i: (0, 0, i, 0)),
            scratch_shapes=[
                pltpu.VMEM((NCHAN * GROUP, 2 * GROUP * NCHAN), jnp.bfloat16),
                pltpu.VMEM((NCHAN * GROUP, 2 * GROUP * NCHAN), jnp.bfloat16),
            ],
        ),
        compiler_params=pltpu.CompilerParams(vmem_limit_bytes=16 << 20),
        cost_estimate=pl.CostEstimate(
            flops=strips * 2 * 2 * 2 * 2 * 256 * 512 * HALF,
            bytes_accessed=strips * 4 * rows * HALF * 2,
            transcendentals=0,
        ),
    )(*args)


def correlate_body(chunk, tiles, sections, place_ref, *refs):
    out_ref, raw, lanes, turned, held, in_sems, add_sems, out_sems = refs[-8:]
    blocks = HALF // PANEL
    frames = lanes.shape[1]
    turn, group = place_ref[0], place_ref[1]

    copies = [
        pltpu.make_async_copy(
            refs[index], raw.at[index // TIMES, index % TIMES], in_sems.at[index]
        )
        for index in range(2 * TIMES)
    ]
    for copy in copies:
        copy.start()

    def earlier(index):
        span = pl.ds(index * PER_STEP, PER_STEP)
        return pltpu.make_async_copy(
            refs[2 * TIMES].at[0, 0, span], held.at[span], add_sems.at[index]
        )

    def repeat(count, action):
        def step(index, carry):
            action(index)
            return carry

        lax.fori_loop(0, count, step, 0)

    if chunk == 1:
        repeat(TSLOT // PER_STEP, lambda index: earlier(index).start())
    for copy in copies:
        copy.wait()

    counts = [sections[0, s] for s in range(N_SITE)]
    starts = [sections[1, s] for s in range(N_SITE)]
    offsets = [jnp.int32(0)]
    for s in range(N_SITE - 1):
        offsets.append(offsets[-1] + counts[s])

    def pick(values, s):
        got = values[0]
        for index in range(1, N_SITE):
            got = jnp.where(s == index, values[index], got)
        return got

    def fill(panel):
        low = panel * PANEL
        high = low + PANEL - 1
        s_low = jnp.int32(0)
        s_high = jnp.int32(0)
        for s in range(1, N_SITE):
            s_low = s_low + (low >= offsets[s]).astype(jnp.int32)
            s_high = s_high + (high >= offsets[s]).astype(jnp.int32)
        bound = jnp.where(s_low == s_high, PANEL, pick(offsets, s_high) - low)
        lane = lax.broadcasted_iota(jnp.int32, (frames, PANEL), 1)

        def piece(s, block, part):
            block = jnp.clip(block, 0, 2 * blocks - 1)
            half = block // blocks
            at = pl.multiple_of((block - half * blocks) * PANEL, PANEL)
            slot = (turn - s + N_SITE) % N_SITE
            values = []
            for which in range(2):
                far = (half + group + which) % 2
                if chunk == 0:
                    value = raw[which, :, 2 * slot + far, part, :, pl.ds(at, PANEL)]
                else:
                    value = raw[which, slot, far, :, part, :, pl.ds(at, PANEL)]
                values.append(value.reshape(frames // 2, PANEL))
            return jnp.concatenate(values, axis=0)

        def window(s, part):
            at = low + pick(starts, s) - pick(offsets, s)
            block, shift = at >> 7, at & 127
            mixed = jnp.where(lane >= shift, piece(s, block, part), piece(s, block + 1, part))
            return pltpu.roll(mixed, (PANEL - shift) & 127, 1)

        def put(part, value):
            lanes[panel, :, part * PANEL : (part + 1) * PANEL] = value
            turned[panel, part * PANEL : (part + 1) * PANEL, :] = value.T

        @pl.when(s_low == s_high)
        def _():
            for part in range(2):
                put(part, window(s_low, part))

        @pl.when(s_low != s_high)
        def _():
            for part in range(2):
                put(part, jnp.where(lane < bound, window(s_low, part), window(s_high, part)))

    repeat(PANELS, fill)
    scale = 1.0 / FB

    def result(at):
        return pltpu.make_async_copy(held.at[at], out_ref.at[0, 0, at], out_sems.at[at])

    def multiply(index):
        if chunk == 1:
            earlier(index).wait()
        for slot in range(PER_STEP):
            at = index * PER_STEP + slot
            left = turned[tiles[group, 0, at]]
            right = lanes[tiles[group, 1, at]]
            gram = jnp.dot(left, right, preferred_element_type=jnp.float32)
            real = (gram[:PANEL, :PANEL] + gram[PANEL:, PANEL:]) * scale
            imag = (gram[PANEL:, :PANEL] - gram[:PANEL, PANEL:]) * scale
            held[at, 0] = real + held[at, 0] if chunk == 1 else real
            held[at, 1] = imag + held[at, 1] if chunk == 1 else imag
        for slot in range(PER_STEP):
            result(index * PER_STEP + slot).start()

    repeat(TSLOT // PER_STEP, multiply)
    repeat(TSLOT, lambda at: result(at).wait())


def correlate_call(tiles, sections, place, pieces, sums):
    chunk, count = len(sums), pieces[0].shape[-2]
    frames = BLOCKS * count
    resident = pl.BlockSpec(memory_space=pltpu.HBM)
    return pl.pallas_call(
        functools.partial(correlate_body, chunk),
        out_shape=jax.ShapeDtypeStruct((1, 1, TSLOT, 2, PANEL, PANEL), jnp.float32),
        grid_spec=pltpu.PrefetchScalarGridSpec(
            num_scalar_prefetch=3,
            grid=(),
            in_specs=[resident] * (2 * TIMES + chunk),
            out_specs=resident,
            scratch_shapes=[
                pltpu.VMEM((2, TIMES) + pieces[0].shape, jnp.bfloat16),
                pltpu.VMEM((PANELS, frames, 2 * PANEL), jnp.bfloat16),
                pltpu.VMEM((PANELS, 2 * PANEL, frames), jnp.bfloat16),
                pltpu.VMEM((TSLOT, 2, PANEL, PANEL), jnp.float32),
                pltpu.SemaphoreType.DMA((2 * TIMES,)),
                pltpu.SemaphoreType.DMA((TSLOT // PER_STEP,)),
                pltpu.SemaphoreType.DMA((TSLOT,)),
            ],
        ),
        input_output_aliases={3 + 2 * TIMES: 0} if chunk else {},
        compiler_params=pltpu.CompilerParams(vmem_limit_bytes=24 << 20),
        cost_estimate=pl.CostEstimate(
            flops=TSLOT * 2 * 256 * 256 * frames,
            bytes_accessed=(1 + chunk) * TSLOT * 2 * PANEL * PANEL * 4 + 4 * frames * N_SITE * CAP,
            transcendentals=0,
        ),
    )(tiles, sections, place, *pieces, *sums)


def move_blocks(keys, sources, shapes, moves):
    def body(key_ref, *refs):
        ins, outs, sems = refs[: len(sources)], refs[len(sources) : -1], refs[-1]

        def at(ref, index):
            where = tuple(key_ref[i[0]] if isinstance(i, tuple) else i for i in index)
            return ref.at[where] if where else ref

        copies = [
            pltpu.make_async_copy(at(ins[i], i_at), at(outs[o], o_at), sems.at[number])
            for number, (i, i_at, o, o_at) in enumerate(moves)
        ]
        for copy in copies:
            copy.start()
        for copy in copies:
            copy.wait()

    return pl.pallas_call(
        body,
        out_shape=[jax.ShapeDtypeStruct(shape, jnp.bfloat16) for shape in shapes],
        grid_spec=pltpu.PrefetchScalarGridSpec(
            num_scalar_prefetch=1,
            grid=(),
            in_specs=[pl.BlockSpec(memory_space=pl.ANY)] * len(sources),
            out_specs=[pl.BlockSpec(memory_space=pl.ANY)] * len(shapes),
            scratch_shapes=[pltpu.SemaphoreType.DMA((len(moves),))],
        ),
        compiler_params=pltpu.CompilerParams(vmem_limit_bytes=1 << 20),
    )(keys, *sources)


def from_behind(value, axis):
    count = lax.axis_size(axis)
    return lax.ppermute(value, axis, [(source, source + 1) for source in range(count - 1)])


def across(turn):
    pairs = []
    for site in range(N_SITE):
        for z in range(8):
            for y in range(TIMES):
                for core in range(2):
                    goal = 2 * ((z // 2 + site + turn) % N_SITE) + ((z + core) % 2)
                    source = (site * NCHAN + z * TIMES + y) * 2 + core
                    pairs.append((source, (z // 2 * NCHAN + goal * TIMES + y) * 2 + core))
    return pairs


def along(step):
    return [(z * TIMES + y, z * TIMES + (y + step) % TIMES) for z in range(8) for y in range(TIMES)]


def swap(piece):
    return lax.ppermute(piece, "grp", [(0, 1), (1, 0)])


def correlator(voltages, taps, sections, tile_list):
    halo = from_behind(voltages[:, -GROUP * NCHAN :], "chan")
    trig = jnp.asarray(trig_rows())
    tap_table = tap_rows(taps)
    site, chan, group = (lax.axis_index(name) for name in ("site", "chan", "grp"))
    z, y = chan // TIMES, chan % TIMES
    place = jnp.stack([(z // 2 - site) % N_SITE, group])
    tiles, section_list = jnp.swapaxes(tile_list, 1, 2), sections.T
    strips = LOCAL // STRIP // 2
    even = [2 * ((z // 2 + site + turn) % N_SITE) for turn in range(N_SITE)]
    mine = [goal + (z + group) % 2 for goal in even]
    theirs = [goal + (z + group + 1) % 2 for goal in even]
    keys = jnp.stack(mine + theirs + [(y + step) % TIMES for step in range(TIMES)])
    everyone = ("site", "chan", "grp")
    block = (2, STRIP * strips, HALF)
    turns, steps = range(N_SITE), range(TIMES)

    def far(payload):
        moved = []
        for turn in turns:
            moved.append(lax.ppermute(payload[turn], everyone, across(turn)))
        return moved

    def near(payload):
        moved = list(payload)
        for step in range(1, TIMES):
            moved[step] = lax.ppermute(payload[step], "chan", along(step))
        return moved

    def blocks(sources, shapes, moves):
        return move_blocks(keys, sources, shapes, moves)

    one = filter_call(trig, tap_table, voltages, None, strips, strips, lambda m: m)
    one = one.reshape((8, TIMES) + block)
    moves = [(0, ((N_SITE + turn,),), 0, (turn,)) for turn in turns]
    given = blocks([one], [(N_SITE, TIMES) + block], moves)[0]
    back = swap(given)
    moves = [(0, ((turn,),), turn, (0,)) for turn in turns]
    moves += [(1, (turn,), turn, (1,)) for turn in turns]
    got = far(blocks([one, back], [(2, TIMES) + block] * N_SITE, moves))
    moves = [
        (turn, (side, (2 * N_SITE + step,)), step, (2 * turn + side,))
        for step in steps
        for turn in turns
        for side in range(2)
    ]
    own_one = near(blocks(got, [(2 * N_SITE,) + block] * TIMES, moves))

    two = filter_call(
        trig, tap_table, voltages, halo, 0, strips, lambda m: m % TIMES * 8 + m // TIMES
    ).reshape((TIMES, 8) + block)
    held = near(
        [
            lax.dynamic_index_in_dim(two, (y + step) % TIMES, 0, keepdims=False)
            for step in steps
        ],
    )
    moves = [
        (step, ((N_SITE + turn,),), 0, (turn, step)) for turn in turns for step in steps
    ]
    given = blocks(held, [(N_SITE, TIMES) + block], moves)[0]
    back = swap(given)
    moves = [(step, ((turn,),), turn, (0, step)) for turn in turns for step in steps]
    moves += [(TIMES, (turn,), turn, (1,)) for turn in turns]
    own_two = far(blocks(held + [back], [(2, TIMES) + block] * N_SITE, moves))

    sums = []
    for own in (own_one, own_two):
        pieces = own + [swap(piece) for piece in own]
        sums = [correlate_call(tiles, section_list, place, pieces, sums)]
    return sums[0]


def solution(mesh):
    in_specs = (P(None, "chan", ("site", "grp")), P(), P(), P())
    out_specs = P("site", "chan", "grp", None, None, None)
    return jax.shard_map(
        correlator, mesh=mesh, in_specs=in_specs, out_specs=out_specs, check_vma=False
    )
```

```python
import functools

import jax
import jax.numpy as jnp
import numpy as np
from jax import lax
from jax.experimental import pallas as pl
from jax.experimental.pallas import tpu as pltpu
from jax.sharding import PartitionSpec as P


NIN = 2048
PANEL = 128
PANELS = NIN // PANEL
NCHAN = 32
N_SITE = 4
LOCAL = 64
BLOCKS = 8
FB = LOCAL * BLOCKS
CAP = 768
HALF = 384
TSLOT = 68
TIMES = 4
PER_STEP = 17
STRIP = 16
GROUP = 8


def trig_rows():
    k = np.arange(NCHAN)
    rows = [np.cos(2.0 * np.pi * (m * k % NCHAN) / NCHAN) for m in range(17)]
    rows += [np.sin(2.0 * np.pi * (m * k % NCHAN) / NCHAN) for m in range(1, 16)]
    return np.tile(np.stack(rows), (1, 2 * GROUP)).astype(np.float32)


def tap_rows(taps):
    flipped = taps[::-1]
    rows = [jnp.pad(flipped, ((j + 1, GROUP - 1 - j), (0, 0))) for j in range(GROUP)]
    return jnp.stack(rows).reshape(GROUP, 2 * GROUP * NCHAN)


def filter_body(slot_of, has_halo, trig_ref, tap_ref, before_ref, now_ref, *rest):
    out_ref, high_ref, low_ref = rest[-3:]

    @pl.when(pl.program_id(0) == 0)
    def _():
        full = (trig_ref[...][:, None, :] * tap_ref[...][None]).reshape(
            NCHAN * GROUP, 2 * GROUP * NCHAN
        )
        high = full.astype(jnp.bfloat16)
        high_ref[...] = high
        low_ref[...] = (full - high.astype(jnp.float32)).astype(jnp.bfloat16)

    step = GROUP * NCHAN
    products = []
    for sub in range(STRIP // GROUP):
        pair = []
        for part in range(2):
            now = now_ref[part]
            if sub == 0:
                before = before_ref[part]
                if has_halo:
                    before = jnp.where(pl.program_id(0) == 0, rest[0][part], before)
                frames = jnp.concatenate([before, now[:step]], axis=0)
            else:
                frames = now
            pair.append(
                jnp.dot(high_ref[...], frames, preferred_element_type=jnp.float32)
                + jnp.dot(low_ref[...], frames, preferred_element_type=jnp.float32)
            )
        products.append(pair)

    def rows(part, index):
        return jnp.concatenate(
            [pair[part][index * GROUP : (index + 1) * GROUP] for pair in products], axis=0
        )

    for m in range(17):
        cos_re, cos_im = rows(0, m), rows(1, m)
        if m in (0, 16):
            out_ref[slot_of(m), 0] = cos_re.astype(jnp.bfloat16)
            out_ref[slot_of(m), 1] = cos_im.astype(jnp.bfloat16)
        else:
            sin_re, sin_im = rows(0, 16 + m), rows(1, 16 + m)
            out_ref[slot_of(m), 0] = (cos_re + sin_im).astype(jnp.bfloat16)
            out_ref[slot_of(m), 1] = (cos_im - sin_re).astype(jnp.bfloat16)
            out_ref[slot_of(NCHAN - m), 0] = (cos_re - sin_im).astype(jnp.bfloat16)
            out_ref[slot_of(NCHAN - m), 1] = (cos_im + sin_re).astype(jnp.bfloat16)


def filter_call(trig, tap_table, voltages, halo, begin, strips, slot_of):
    rows = STRIP * NCHAN
    half_rows = GROUP * NCHAN
    in_specs = [
        pl.BlockSpec((NCHAN, 2 * GROUP * NCHAN), lambda i: (0, 0)),
        pl.BlockSpec((GROUP, 2 * GROUP * NCHAN), lambda i: (0, 0)),
        pl.BlockSpec((2, half_rows, HALF), lambda i: (0, jnp.maximum(2 * (i + begin) - 1, 0), 0)),
        pl.BlockSpec((2, rows, HALF), lambda i: (0, i + begin, 0)),
    ]
    args = [trig, tap_table, voltages, voltages]
    if halo is not None:
        in_specs.append(pl.BlockSpec((2, half_rows, HALF), lambda i: (0, 0, 0)))
        args.append(halo)
    return pl.pallas_call(
        functools.partial(filter_body, slot_of, halo is not None),
        out_shape=jax.ShapeDtypeStruct((NCHAN, 2, STRIP * strips, HALF), jnp.bfloat16),
        grid_spec=pltpu.PrefetchScalarGridSpec(
            num_scalar_prefetch=0,
            grid=(strips,),
            in_specs=in_specs,
            out_specs=pl.BlockSpec((NCHAN, 2, STRIP, HALF), lambda i: (0, 0, i, 0)),
            scratch_shapes=[
                pltpu.VMEM((NCHAN * GROUP, 2 * GROUP * NCHAN), jnp.bfloat16),
                pltpu.VMEM((NCHAN * GROUP, 2 * GROUP * NCHAN), jnp.bfloat16),
            ],
        ),
        compiler_params=pltpu.CompilerParams(vmem_limit_bytes=(16 if halo is not None else 60) << 20),
        cost_estimate=pl.CostEstimate(
            flops=strips * 2 * 2 * 2 * 2 * 256 * 512 * HALF,
            bytes_accessed=strips * 4 * rows * HALF * 2,
            transcendentals=0,
        ),
    )(*args)


def correlate_body(chunk, tiles, sections, place_ref, *refs):
    out_ref, raw, lanes, held, in_sems, add_sems, out_sems = refs[-7:]
    blocks = HALF // PANEL
    frames = lanes.shape[1]
    turn, group = place_ref[0], place_ref[1]

    copies = [
        pltpu.make_async_copy(
            refs[index], raw.at[index // TIMES, index % TIMES], in_sems.at[index]
        )
        for index in range(2 * TIMES)
    ]
    for copy in copies:
        copy.start()

    def earlier(index):
        span = pl.ds(index * PER_STEP, PER_STEP)
        return pltpu.make_async_copy(
            refs[2 * TIMES].at[0, 0, span], held.at[span], add_sems.at[index]
        )

    def repeat(count, action):
        def step(index, carry):
            action(index)
            return carry

        lax.fori_loop(0, count, step, 0)

    if chunk == 1:
        repeat(TSLOT // PER_STEP, lambda index: earlier(index).start())
    for copy in copies:
        copy.wait()

    counts = [sections[0, s] for s in range(N_SITE)]
    starts = [sections[1, s] for s in range(N_SITE)]
    offsets = [jnp.int32(0)]
    for s in range(N_SITE - 1):
        offsets.append(offsets[-1] + counts[s])

    def pick(values, s):
        got = values[0]
        for index in range(1, N_SITE):
            got = jnp.where(s == index, values[index], got)
        return got

    def fill(panel):
        low = panel * PANEL
        high = low + PANEL - 1
        s_low = jnp.int32(0)
        s_high = jnp.int32(0)
        for s in range(1, N_SITE):
            s_low = s_low + (low >= offsets[s]).astype(jnp.int32)
            s_high = s_high + (high >= offsets[s]).astype(jnp.int32)
        bound = jnp.where(s_low == s_high, PANEL, pick(offsets, s_high) - low)
        lane = lax.broadcasted_iota(jnp.int32, (frames, PANEL), 1)

        def piece(s, block, part):
            block = jnp.clip(block, 0, 2 * blocks - 1)
            half = block // blocks
            at = pl.multiple_of((block - half * blocks) * PANEL, PANEL)
            slot = (turn - s + N_SITE) % N_SITE
            values = []
            for which in range(2):
                far = (half + group + which) % 2
                if chunk == 0:
                    value = raw[which, :, 2 * slot + far, part, :, pl.ds(at, PANEL)]
                else:
                    value = raw[which, slot, far, :, part, :, pl.ds(at, PANEL)]
                values.append(value.reshape(frames // 2, PANEL))
            return jnp.concatenate(values, axis=0)

        def window(s, part):
            at = low + pick(starts, s) - pick(offsets, s)
            block, shift = at >> 7, at & 127
            mixed = jnp.where(lane >= shift, piece(s, block, part), piece(s, block + 1, part))
            return pltpu.roll(mixed, (PANEL - shift) & 127, 1)

        def put(part, value):
            lanes[panel, :, part * PANEL : (part + 1) * PANEL] = value

        @pl.when(s_low == s_high)
        def _():
            for part in range(2):
                put(part, window(s_low, part))

        @pl.when(s_low != s_high)
        def _():
            for part in range(2):
                put(part, jnp.where(lane < bound, window(s_low, part), window(s_high, part)))

    repeat(PANELS, fill)
    scale = 1.0 / FB

    def result(at):
        return pltpu.make_async_copy(held.at[at], out_ref.at[0, 0, at], out_sems.at[at])

    def multiply(index):
        if chunk == 1:
            earlier(index).wait()
        for slot in range(PER_STEP):
            at = index * PER_STEP + slot
            left = lanes[tiles[group, 0, at]]
            right = lanes[tiles[group, 1, at]]
            gram = lax.dot_general(
                left, right, (((0,), (0,)), ((), ())), preferred_element_type=jnp.float32
            )
            real = (gram[:PANEL, :PANEL] + gram[PANEL:, PANEL:]) * scale
            imag = (gram[PANEL:, :PANEL] - gram[:PANEL, PANEL:]) * scale
            held[at, 0] = real + held[at, 0] if chunk == 1 else real
            held[at, 1] = imag + held[at, 1] if chunk == 1 else imag
        for slot in range(PER_STEP):
            result(index * PER_STEP + slot).start()

    repeat(TSLOT // PER_STEP, multiply)
    repeat(TSLOT, lambda at: result(at).wait())


def correlate_call(tiles, sections, place, pieces, sums):
    chunk, count = len(sums), pieces[0].shape[-2]
    frames = BLOCKS * count
    resident = pl.BlockSpec(memory_space=pltpu.HBM)
    return pl.pallas_call(
        functools.partial(correlate_body, chunk),
        out_shape=jax.ShapeDtypeStruct((1, 1, TSLOT, 2, PANEL, PANEL), jnp.float32),
        grid_spec=pltpu.PrefetchScalarGridSpec(
            num_scalar_prefetch=3,
            grid=(),
            in_specs=[resident] * (2 * TIMES + chunk),
            out_specs=resident,
            scratch_shapes=[
                pltpu.VMEM((2, TIMES) + pieces[0].shape, jnp.bfloat16),
                pltpu.VMEM((PANELS, frames, 2 * PANEL), jnp.bfloat16),
                pltpu.VMEM((TSLOT, 2, PANEL, PANEL), jnp.float32),
                pltpu.SemaphoreType.DMA((2 * TIMES,)),
                pltpu.SemaphoreType.DMA((TSLOT // PER_STEP,)),
                pltpu.SemaphoreType.DMA((TSLOT,)),
            ],
        ),
        input_output_aliases={3 + 2 * TIMES: 0} if chunk else {},
        compiler_params=pltpu.CompilerParams(vmem_limit_bytes=24 << 20),
        cost_estimate=pl.CostEstimate(
            flops=TSLOT * 2 * 256 * 256 * frames,
            bytes_accessed=(1 + chunk) * TSLOT * 2 * PANEL * PANEL * 4 + 4 * frames * N_SITE * CAP,
            transcendentals=0,
        ),
    )(tiles, sections, place, *pieces, *sums)


def move_blocks(keys, sources, shapes, moves):
    def body(key_ref, *refs):
        ins, outs, sems = refs[: len(sources)], refs[len(sources) : -1], refs[-1]

        def at(ref, index):
            where = tuple(key_ref[i[0]] if isinstance(i, tuple) else i for i in index)
            return ref.at[where] if where else ref

        copies = [
            pltpu.make_async_copy(at(ins[i], i_at), at(outs[o], o_at), sems.at[number])
            for number, (i, i_at, o, o_at) in enumerate(moves)
        ]
        for copy in copies:
            copy.start()
        for copy in copies:
            copy.wait()

    return pl.pallas_call(
        body,
        out_shape=[jax.ShapeDtypeStruct(shape, jnp.bfloat16) for shape in shapes],
        grid_spec=pltpu.PrefetchScalarGridSpec(
            num_scalar_prefetch=1,
            grid=(),
            in_specs=[pl.BlockSpec(memory_space=pl.ANY)] * len(sources),
            out_specs=[pl.BlockSpec(memory_space=pl.ANY)] * len(shapes),
            scratch_shapes=[pltpu.SemaphoreType.DMA((len(moves),))],
        ),
        compiler_params=pltpu.CompilerParams(vmem_limit_bytes=1 << 20),
    )(keys, *sources)


def from_behind(value, axis):
    count = lax.axis_size(axis)
    return lax.ppermute(value, axis, [(source, source + 1) for source in range(count - 1)])


def across(turn):
    pairs = []
    for site in range(N_SITE):
        for z in range(8):
            for y in range(TIMES):
                for core in range(2):
                    goal = 2 * ((z // 2 + site + turn) % N_SITE) + ((z + core) % 2)
                    source = (site * NCHAN + z * TIMES + y) * 2 + core
                    pairs.append((source, (z // 2 * NCHAN + goal * TIMES + y) * 2 + core))
    return pairs


def along(step):
    return [(z * TIMES + y, z * TIMES + (y + step) % TIMES) for z in range(8) for y in range(TIMES)]


def swap(piece):
    return lax.ppermute(piece, "grp", [(0, 1), (1, 0)])


def correlator(voltages, taps, sections, tile_list):
    halo = from_behind(voltages[:, -GROUP * NCHAN :], "chan")
    trig = jnp.asarray(trig_rows())
    tap_table = tap_rows(taps)
    site, chan, group = (lax.axis_index(name) for name in ("site", "chan", "grp"))
    z, y = chan // TIMES, chan % TIMES
    place = jnp.stack([(z // 2 - site) % N_SITE, group])
    tiles, section_list = jnp.swapaxes(tile_list, 1, 2), sections.T
    strips = LOCAL // STRIP // 2
    even = [2 * ((z // 2 + site + turn) % N_SITE) for turn in range(N_SITE)]
    mine = [goal + (z + group) % 2 for goal in even]
    theirs = [goal + (z + group + 1) % 2 for goal in even]
    keys = jnp.stack(mine + theirs + [(y + step) % TIMES for step in range(TIMES)])
    everyone = ("site", "chan", "grp")
    block = (2, STRIP * strips, HALF)
    turns, steps = range(N_SITE), range(TIMES)

    def far(payload):
        moved = []
        for turn in turns:
            moved.append(lax.ppermute(payload[turn], everyone, across(turn)))
        return moved

    def near(payload):
        moved = list(payload)
        for step in range(1, TIMES):
            moved[step] = lax.ppermute(payload[step], "chan", along(step))
        return moved

    def blocks(sources, shapes, moves):
        return move_blocks(keys, sources, shapes, moves)

    one = filter_call(trig, tap_table, voltages, None, strips, strips, lambda m: m)
    one = one.reshape((8, TIMES) + block)
    moves = [(0, ((N_SITE + turn,),), 0, (turn,)) for turn in turns]
    given = blocks([one], [(N_SITE, TIMES) + block], moves)[0]
    back = swap(given)
    moves = [(0, ((turn,),), turn, (0,)) for turn in turns]
    moves += [(1, (turn,), turn, (1,)) for turn in turns]
    got = far(blocks([one, back], [(2, TIMES) + block] * N_SITE, moves))
    moves = [
        (turn, (side, (2 * N_SITE + step,)), step, (2 * turn + side,))
        for step in steps
        for turn in turns
        for side in range(2)
    ]
    own_one = near(blocks(got, [(2 * N_SITE,) + block] * TIMES, moves))

    two = filter_call(
        trig, tap_table, voltages, halo, 0, strips, lambda m: m % TIMES * 8 + m // TIMES
    ).reshape((TIMES, 8) + block)
    held = near(
        [
            lax.dynamic_index_in_dim(two, (y + step) % TIMES, 0, keepdims=False)
            for step in steps
        ],
    )
    moves = [
        (step, ((N_SITE + turn,),), 0, (turn, step)) for turn in turns for step in steps
    ]
    given = blocks(held, [(N_SITE, TIMES) + block], moves)[0]
    back = swap(given)
    moves = [(step, ((turn,),), turn, (0, step)) for turn in turns for step in steps]
    moves += [(TIMES, (turn,), turn, (1,)) for turn in turns]
    own_two = far(blocks(held + [back], [(2, TIMES) + block] * N_SITE, moves))

    sums = []
    for own in (own_one, own_two):
        pieces = own + [swap(piece) for piece in own]
        sums = [correlate_call(tiles, section_list, place, pieces, sums)]
    return sums[0]


def solution(mesh):
    in_specs = (P(None, "chan", ("site", "grp")), P(), P(), P())
    out_specs = P("site", "chan", "grp", None, None, None)
    return jax.shard_map(
        correlator, mesh=mesh, in_specs=in_specs, out_specs=out_specs, check_vma=False
    )
```

```python
import functools

import jax
import jax.numpy as jnp
import numpy as np
from jax import lax
from jax.experimental import pallas as pl
from jax.experimental.pallas import tpu as pltpu
from jax.sharding import PartitionSpec as P


NIN = 2048
PANEL = 128
PANELS = NIN // PANEL
NCHAN = 32
N_SITE = 4
LOCAL = 64
BLOCKS = 8
FB = LOCAL * BLOCKS
CAP = 768
HALF = 384
TSLOT = 68
TIMES = 4
PER_STEP = 17
STRIP = 16
GROUP = 8


def trig_rows():
    k = np.arange(NCHAN)
    rows = [np.cos(2.0 * np.pi * (m * k % NCHAN) / NCHAN) for m in range(17)]
    rows += [np.sin(2.0 * np.pi * (m * k % NCHAN) / NCHAN) for m in range(1, 16)]
    return np.tile(np.stack(rows), (1, 2 * GROUP)).astype(np.float32)


def tap_rows(taps):
    flipped = taps[::-1]
    rows = [jnp.pad(flipped, ((j + 1, GROUP - 1 - j), (0, 0))) for j in range(GROUP)]
    return jnp.stack(rows).reshape(GROUP, 2 * GROUP * NCHAN)


def filter_body(slot_of, has_halo, trig_ref, tap_ref, before_ref, now_ref, *rest):
    out_ref, high_ref, low_ref = rest[-3:]

    @pl.when(pl.program_id(0) == 0)
    def _():
        full = (trig_ref[...][:, None, :] * tap_ref[...][None]).reshape(
            NCHAN * GROUP, 2 * GROUP * NCHAN
        )
        high = full.astype(jnp.bfloat16)
        high_ref[...] = high
        low_ref[...] = (full - high.astype(jnp.float32)).astype(jnp.bfloat16)

    step = GROUP * NCHAN
    products = []
    for sub in range(STRIP // GROUP):
        pair = []
        for part in range(2):
            now = now_ref[part]
            if sub == 0:
                before = before_ref[part]
                if has_halo:
                    before = jnp.where(pl.program_id(0) == 0, rest[0][part], before)
                frames = jnp.concatenate([before, now[:step]], axis=0)
            else:
                frames = now
            pair.append(
                jnp.dot(high_ref[...], frames, preferred_element_type=jnp.float32)
                + jnp.dot(low_ref[...], frames, preferred_element_type=jnp.float32)
            )
        products.append(pair)

    def rows(part, index):
        return jnp.concatenate(
            [pair[part][index * GROUP : (index + 1) * GROUP] for pair in products], axis=0
        )

    for m in range(17):
        cos_re, cos_im = rows(0, m), rows(1, m)
        if m in (0, 16):
            out_ref[slot_of(m), 0] = cos_re.astype(jnp.bfloat16)
            out_ref[slot_of(m), 1] = cos_im.astype(jnp.bfloat16)
        else:
            sin_re, sin_im = rows(0, 16 + m), rows(1, 16 + m)
            out_ref[slot_of(m), 0] = (cos_re + sin_im).astype(jnp.bfloat16)
            out_ref[slot_of(m), 1] = (cos_im - sin_re).astype(jnp.bfloat16)
            out_ref[slot_of(NCHAN - m), 0] = (cos_re - sin_im).astype(jnp.bfloat16)
            out_ref[slot_of(NCHAN - m), 1] = (cos_im + sin_re).astype(jnp.bfloat16)


def filter_call(trig, tap_table, voltages, halo, begin, strips, slot_of):
    rows = STRIP * NCHAN
    half_rows = GROUP * NCHAN
    in_specs = [
        pl.BlockSpec((NCHAN, 2 * GROUP * NCHAN), lambda i: (0, 0)),
        pl.BlockSpec((GROUP, 2 * GROUP * NCHAN), lambda i: (0, 0)),
        pl.BlockSpec((2, half_rows, HALF), lambda i: (0, jnp.maximum(2 * (i + begin) - 1, 0), 0)),
        pl.BlockSpec((2, rows, HALF), lambda i: (0, i + begin, 0)),
    ]
    args = [trig, tap_table, voltages, voltages]
    if halo is not None:
        in_specs.append(pl.BlockSpec((2, half_rows, HALF), lambda i: (0, 0, 0)))
        args.append(halo)
    return pl.pallas_call(
        functools.partial(filter_body, slot_of, halo is not None),
        out_shape=jax.ShapeDtypeStruct((NCHAN, 2, STRIP * strips, HALF), jnp.bfloat16),
        grid_spec=pltpu.PrefetchScalarGridSpec(
            num_scalar_prefetch=0,
            grid=(strips,),
            in_specs=in_specs,
            out_specs=pl.BlockSpec((NCHAN, 2, STRIP, HALF), lambda i: (0, 0, i, 0)),
            scratch_shapes=[
                pltpu.VMEM((NCHAN * GROUP, 2 * GROUP * NCHAN), jnp.bfloat16),
                pltpu.VMEM((NCHAN * GROUP, 2 * GROUP * NCHAN), jnp.bfloat16),
            ],
        ),
        compiler_params=pltpu.CompilerParams(vmem_limit_bytes=(16 if halo is not None else 60) << 20),
        cost_estimate=pl.CostEstimate(
            flops=strips * 2 * 2 * 2 * 2 * 256 * 512 * HALF,
            bytes_accessed=strips * 4 * rows * HALF * 2,
            transcendentals=0,
        ),
    )(*args)


def correlate_body(chunk, tiles, sections, place_ref, *refs):
    out_ref, raw, lanes, held, in_sems, add_sems, out_sems = refs[-7:]
    blocks = HALF // PANEL
    frames = lanes.shape[1]
    turn, group = place_ref[0], place_ref[1]

    copies = [
        pltpu.make_async_copy(
            refs[index], raw.at[index // TIMES, index % TIMES], in_sems.at[index]
        )
        for index in range(2 * TIMES)
    ]
    for copy in copies:
        copy.start()

    def earlier(index):
        span = pl.ds(index * PER_STEP, PER_STEP)
        return pltpu.make_async_copy(
            refs[2 * TIMES].at[0, 0, span], held.at[span], add_sems.at[index]
        )

    def repeat(count, action):
        def step(index, carry):
            action(index)
            return carry

        lax.fori_loop(0, count, step, 0)

    if chunk == 1:
        repeat(TSLOT // PER_STEP, lambda index: earlier(index).start())
    for copy in copies:
        copy.wait()

    counts = [sections[0, s] for s in range(N_SITE)]
    starts = [sections[1, s] for s in range(N_SITE)]
    offsets = [jnp.int32(0)]
    for s in range(N_SITE - 1):
        offsets.append(offsets[-1] + counts[s])

    def pick(values, s):
        got = values[0]
        for index in range(1, N_SITE):
            got = jnp.where(s == index, values[index], got)
        return got

    def fill(panel):
        low = panel * PANEL
        high = low + PANEL - 1
        s_low = jnp.int32(0)
        s_high = jnp.int32(0)
        for s in range(1, N_SITE):
            s_low = s_low + (low >= offsets[s]).astype(jnp.int32)
            s_high = s_high + (high >= offsets[s]).astype(jnp.int32)
        bound = jnp.where(s_low == s_high, PANEL, pick(offsets, s_high) - low)
        lane = lax.broadcasted_iota(jnp.int32, (frames, PANEL), 1)

        def piece(s, block, part):
            block = jnp.clip(block, 0, 2 * blocks - 1)
            half = block // blocks
            at = pl.multiple_of((block - half * blocks) * PANEL, PANEL)
            slot = (turn - s + N_SITE) % N_SITE
            values = []
            for which in range(2):
                far = (half + group + which) % 2
                if chunk == 0:
                    value = raw[which, :, 2 * slot + far, part, :, pl.ds(at, PANEL)]
                else:
                    value = raw[which, slot, far, :, part, :, pl.ds(at, PANEL)]
                values.append(value.reshape(frames // 2, PANEL))
            return jnp.concatenate(values, axis=0)

        def window(s, part):
            at = low + pick(starts, s) - pick(offsets, s)
            block, shift = at >> 7, at & 127
            mixed = jnp.where(lane >= shift, piece(s, block, part), piece(s, block + 1, part))
            return pltpu.roll(mixed, (PANEL - shift) & 127, 1)

        def put(part, value):
            lanes[panel, :, part * PANEL : (part + 1) * PANEL] = value

        @pl.when(s_low == s_high)
        def _():
            for part in range(2):
                put(part, window(s_low, part))

        @pl.when(s_low != s_high)
        def _():
            for part in range(2):
                put(part, jnp.where(lane < bound, window(s_low, part), window(s_high, part)))

    repeat(PANELS, fill)
    scale = 1.0 / FB

    def result(at):
        return pltpu.make_async_copy(held.at[at], out_ref.at[0, 0, at], out_sems.at[at])

    def multiply(index):
        if chunk == 1:
            earlier(index).wait()
        for slot in range(PER_STEP):
            at = index * PER_STEP + slot
            left = lanes[tiles[group, 0, at]]
            right = lanes[tiles[group, 1, at]]
            gram = lax.dot_general(
                left, right, (((0,), (0,)), ((), ())), preferred_element_type=jnp.float32
            )
            real = (gram[:PANEL, :PANEL] + gram[PANEL:, PANEL:]) * scale
            imag = (gram[PANEL:, :PANEL] - gram[:PANEL, PANEL:]) * scale
            held[at, 0] = real + held[at, 0] if chunk == 1 else real
            held[at, 1] = imag + held[at, 1] if chunk == 1 else imag
            if slot in (PER_STEP // 2, PER_STEP - 1):
                first = 0 if slot < PER_STEP - 1 else PER_STEP // 2 + 1
                for done in range(first, slot + 1):
                    result(index * PER_STEP + done).start()

    repeat(TSLOT // PER_STEP, multiply)
    repeat(TSLOT, lambda at: result(at).wait())


def correlate_call(tiles, sections, place, pieces, sums):
    chunk, count = len(sums), pieces[0].shape[-2]
    frames = BLOCKS * count
    resident = pl.BlockSpec(memory_space=pltpu.HBM)
    return pl.pallas_call(
        functools.partial(correlate_body, chunk),
        out_shape=jax.ShapeDtypeStruct((1, 1, TSLOT, 2, PANEL, PANEL), jnp.float32),
        grid_spec=pltpu.PrefetchScalarGridSpec(
            num_scalar_prefetch=3,
            grid=(),
            in_specs=[resident] * (2 * TIMES + chunk),
            out_specs=resident,
            scratch_shapes=[
                pltpu.VMEM((2, TIMES) + pieces[0].shape, jnp.bfloat16),
                pltpu.VMEM((PANELS, frames, 2 * PANEL), jnp.bfloat16),
                pltpu.VMEM((TSLOT, 2, PANEL, PANEL), jnp.float32),
                pltpu.SemaphoreType.DMA((2 * TIMES,)),
                pltpu.SemaphoreType.DMA((TSLOT // PER_STEP,)),
                pltpu.SemaphoreType.DMA((TSLOT,)),
            ],
        ),
        input_output_aliases={3 + 2 * TIMES: 0} if chunk else {},
        compiler_params=pltpu.CompilerParams(vmem_limit_bytes=24 << 20),
        cost_estimate=pl.CostEstimate(
            flops=TSLOT * 2 * 256 * 256 * frames,
            bytes_accessed=(1 + chunk) * TSLOT * 2 * PANEL * PANEL * 4 + 4 * frames * N_SITE * CAP,
            transcendentals=0,
        ),
    )(tiles, sections, place, *pieces, *sums)


def move_blocks(keys, sources, shapes, moves):
    def body(key_ref, *refs):
        ins, outs, sems = refs[: len(sources)], refs[len(sources) : -1], refs[-1]

        def at(ref, index):
            where = tuple(key_ref[i[0]] if isinstance(i, tuple) else i for i in index)
            return ref.at[where] if where else ref

        copies = [
            pltpu.make_async_copy(at(ins[i], i_at), at(outs[o], o_at), sems.at[number])
            for number, (i, i_at, o, o_at) in enumerate(moves)
        ]
        for copy in copies:
            copy.start()
        for copy in copies:
            copy.wait()

    return pl.pallas_call(
        body,
        out_shape=[jax.ShapeDtypeStruct(shape, jnp.bfloat16) for shape in shapes],
        grid_spec=pltpu.PrefetchScalarGridSpec(
            num_scalar_prefetch=1,
            grid=(),
            in_specs=[pl.BlockSpec(memory_space=pl.ANY)] * len(sources),
            out_specs=[pl.BlockSpec(memory_space=pl.ANY)] * len(shapes),
            scratch_shapes=[pltpu.SemaphoreType.DMA((len(moves),))],
        ),
        compiler_params=pltpu.CompilerParams(vmem_limit_bytes=1 << 20),
    )(keys, *sources)


def from_behind(value, axis):
    count = lax.axis_size(axis)
    return lax.ppermute(value, axis, [(source, source + 1) for source in range(count - 1)])


def across(turn):
    pairs = []
    for site in range(N_SITE):
        for z in range(8):
            for y in range(TIMES):
                for core in range(2):
                    goal = 2 * ((z // 2 + site + turn) % N_SITE) + ((z + core) % 2)
                    source = (site * NCHAN + z * TIMES + y) * 2 + core
                    pairs.append((source, (z // 2 * NCHAN + goal * TIMES + y) * 2 + core))
    return pairs


def along(step):
    return [(z * TIMES + y, z * TIMES + (y + step) % TIMES) for z in range(8) for y in range(TIMES)]


def swap(piece):
    return lax.ppermute(piece, "grp", [(0, 1), (1, 0)])


def correlator(voltages, taps, sections, tile_list):
    halo = from_behind(voltages[:, -GROUP * NCHAN :], "chan")
    trig = jnp.asarray(trig_rows())
    tap_table = tap_rows(taps)
    site, chan, group = (lax.axis_index(name) for name in ("site", "chan", "grp"))
    z, y = chan // TIMES, chan % TIMES
    place = jnp.stack([(z // 2 - site) % N_SITE, group])
    tiles, section_list = jnp.swapaxes(tile_list, 1, 2), sections.T
    strips = LOCAL // STRIP // 2
    even = [2 * ((z // 2 + site + turn) % N_SITE) for turn in range(N_SITE)]
    mine = [goal + (z + group) % 2 for goal in even]
    theirs = [goal + (z + group + 1) % 2 for goal in even]
    keys = jnp.stack(mine + theirs + [(y + step) % TIMES for step in range(TIMES)])
    everyone = ("site", "chan", "grp")
    block = (2, STRIP * strips, HALF)
    turns, steps = range(N_SITE), range(TIMES)

    def far(payload):
        moved = []
        for turn in turns:
            moved.append(lax.ppermute(payload[turn], everyone, across(turn)))
        return moved

    def near(payload):
        moved = list(payload)
        for step in range(1, TIMES):
            moved[step] = lax.ppermute(payload[step], "chan", along(step))
        return moved

    def blocks(sources, shapes, moves):
        return move_blocks(keys, sources, shapes, moves)

    one = filter_call(trig, tap_table, voltages, None, strips, strips, lambda m: m)
    one = one.reshape((8, TIMES) + block)
    moves = [(0, ((N_SITE + turn,),), 0, (turn,)) for turn in turns]
    given = blocks([one], [(N_SITE, TIMES) + block], moves)[0]
    back = swap(given)
    moves = [(0, ((turn,),), turn, (0,)) for turn in turns]
    moves += [(1, (turn,), turn, (1,)) for turn in turns]
    got = far(blocks([one, back], [(2, TIMES) + block] * N_SITE, moves))
    moves = [
        (turn, (side, (2 * N_SITE + step,)), step, (2 * turn + side,))
        for step in steps
        for turn in turns
        for side in range(2)
    ]
    own_one = near(blocks(got, [(2 * N_SITE,) + block] * TIMES, moves))

    two = filter_call(
        trig, tap_table, voltages, halo, 0, strips, lambda m: m % TIMES * 8 + m // TIMES
    ).reshape((TIMES, 8) + block)
    held = near(
        [
            lax.dynamic_index_in_dim(two, (y + step) % TIMES, 0, keepdims=False)
            for step in steps
        ],
    )
    moves = [
        (step, ((N_SITE + turn,),), 0, (turn, step)) for turn in turns for step in steps
    ]
    given = blocks(held, [(N_SITE, TIMES) + block], moves)[0]
    back = swap(given)
    moves = [(step, ((turn,),), turn, (0, step)) for turn in turns for step in steps]
    moves += [(TIMES, (turn,), turn, (1,)) for turn in turns]
    own_two = far(blocks(held + [back], [(2, TIMES) + block] * N_SITE, moves))

    sums = []
    for own in (own_one, own_two):
        pieces = own + [swap(piece) for piece in own]
        sums = [correlate_call(tiles, section_list, place, pieces, sums)]
    return sums[0]


def solution(mesh):
    in_specs = (P(None, "chan", ("site", "grp")), P(), P(), P())
    out_specs = P("site", "chan", "grp", None, None, None)
    return jax.shard_map(
        correlator, mesh=mesh, in_specs=in_specs, out_specs=out_specs, check_vma=False
    )
```
